32 devices in a mesh: kpt: 4 (over y, core), row: 4 (over z), col: 2 (over x).
Axes of the slice: x: 2, y: 2, z: 4, core: 2. Of those that a mesh axis runs over, the one named last changes fastest.
Arguments:
- a_matrix: bfloat16 [8, 4096, 4096], P('kpt', 'row', 'col'), parts along dimension 0, may hold values from -6 to 6
- b_matrix: bfloat16 [8, 4096, 4096], P('kpt', 'row', 'col'), parts along dimension 0, may hold values from -0.09375 to 0.09375
- a_level: int32 [128, 32], P('kpt'), parts along dimension 0, may hold values from 0 to 4, as said below
- b_level: int32 [128, 32], P('kpt'), parts along dimension 0, may hold values from 0 to 4, as said below
- limit: int32 [128, 32], P(('kpt', 'row'), 'col'), parts along dimension 0, may hold values from 3 to 8
Outputs:
- product: bfloat16 [8, 4096, 4096], P('kpt', 'row', 'col'), parts along dimension 0
- kept_count: int32 [128, 32], P(('kpt', 'row'), 'col'), parts along dimension 0
- kept_total: int32 [4], P('kpt'), parts along dimension 0
The draws below stay inside these ranges and needn't reach their ends.
There are 4 independent parts, one for each index of `kpt`. The reference program is written for one: setup_inputs(seed, part) draws one part's arguments, and reference() takes and returns one part's arrays. A program takes and returns all parts, laid end to end along the dimension named above; each array names one. Nothing has to cross between parts.
Inputs may be any that keep to these rules, and one draw needn't show every extreme that they name: Each block's level is 0 (empty) or its norm exponent 1 to 4; the share of occupied blocks rises from some a sixth in the first block row of a_level (block column of b_level) to some six in seven in the last. `b_level`: as for a_level, with the share rising along block columns.
All inputs are finite; a program needn't handle non-finite values.
Results may differ from the reference program's by a relative error of at most 0.001.
Values may be sent and summed in bfloat16 or wider, within the bound.
No kernel may reach another device: no remote copies, remote signals or barrier semaphores. Data moves between devices by JAX's collectives and lax.ppermute only.
A program may use at most 576 MiB of HBM per device.

```python
import jax
import jax.numpy as jnp
from jax import lax

ORDER = 4096
BLK = 128
NBLK = 32


def skewed_levels(key, along_rows):
    first, second = jax.random.split(jax.random.fold_in(key, 71))
    chance = jax.random.randint(first, (NBLK, NBLK), 0, 100)
    level = jax.random.randint(second, (NBLK, NBLK), 1, 5)
    steps = jnp.arange(NBLK, dtype=jnp.int32)
    percent = 15 + 70 * steps // (NBLK - 1)
    bound = percent[:, None] if along_rows else percent[None, :]
    return jnp.where(chance < bound, level, 0).astype(jnp.int32)


def draw_a_level(key, part):
    return skewed_levels(jax.random.fold_in(key, 3), True)


def draw_b_level(key, part):
    return skewed_levels(jax.random.fold_in(key, 5), False)


def touch_ends(entries, rng, smallest, largest):
    longest = entries.shape.index(max(entries.shape))
    spots = []
    for shift in (0, 1):
        where = [jax.random.randint(jax.random.fold_in(rng, axis), (), 0, length) for axis, length in enumerate(entries.shape)]
        where[longest] = (where[longest] + shift) % entries.shape[longest]
        spots.append(tuple(where))
    return entries.at[spots[0]].set(smallest).at[spots[1]].set(largest)


def level_of(rng, dims, cuts, least, top_value):
    level = 1.0
    for axis_at, parts in cuts:
        heights = jax.random.uniform(jax.random.fold_in(jax.random.fold_in(rng, 6), axis_at), (parts,), jnp.float32, least / len(cuts), top_value / len(cuts))
        level = level * jnp.repeat(jnp.exp(heights), dims[axis_at] // parts).reshape((-1,) + (1,) * (len(dims) - 1 - axis_at))
    return level


def normal_values(key, dims, spread, most, cuts=(), kind=jnp.bfloat16):
    values = jax.random.normal(key, dims, jnp.float32) * spread
    if len(cuts) > 0:
        values = level_of(key, dims, cuts, -0.22, 0.18) * values
    return jnp.clip(values, min=-most, max=most).astype(kind)


def setup_inputs(seed: int = 0, part: int = 0) -> dict:
    key_of = jax.random.split(jax.random.key(seed), 6)
    part_splits = jax.random.split(jax.random.fold_in(key_of[5], part), 6)
    a_matrix = normal_values(part_splits[0], (2, ORDER, ORDER), 1.0, 6.0, ((1, 4), (2, 2)))
    b_matrix = normal_values(part_splits[1], (2, ORDER, ORDER), ORDER ** -0.5, 0.09375, ((1, 4), (2, 2)))
    a_level = draw_a_level(jax.random.fold_in(jax.random.fold_in(key_of[5], part), 71), part)
    b_level = draw_b_level(jax.random.fold_in(jax.random.fold_in(key_of[5], part), 71), part)
    limit = touch_ends(jax.random.randint(part_splits[4], (NBLK, NBLK), 3, 9), jax.random.fold_in(part_splits[4], 1), 3, 8).astype(jnp.int32)
    return {"a_matrix": a_matrix, "b_matrix": b_matrix, "a_level": a_level, "b_level": b_level, "limit": limit}


def level_scale(levels):
    power = jnp.power(jnp.float32(2.0), (1 - levels).astype(jnp.float32))
    return jnp.where(levels > 0, power, jnp.float32(0.0))


def spread_blocks(small):
    return jnp.repeat(jnp.repeat(small, BLK, axis=0), BLK, axis=1)


def reference(a_matrix, b_matrix, a_level, b_level, limit):
    a_eff = a_matrix * spread_blocks(level_scale(a_level)).astype(jnp.bfloat16)[None]
    b_eff = b_matrix * spread_blocks(level_scale(b_level)).astype(jnp.bfloat16)[None]
    keep = (a_level[:, :, None] > 0) & (b_level[None, :, :] > 0) & (a_level[:, :, None] + b_level[None, :, :] <= limit[:, None, :])
    kept_count = jnp.sum(keep.astype(jnp.int32), axis=1).astype(jnp.int32)
    kept_total = jnp.sum(kept_count).reshape(1).astype(jnp.int32)

    def one_column(index):
        mask = spread_blocks(lax.dynamic_index_in_dim(keep, index, 2, keepdims=False))
        masked = jnp.where(mask[None], a_eff, jnp.zeros((), jnp.bfloat16))
        column = lax.dynamic_slice_in_dim(b_eff, (index * BLK).astype(jnp.int32), BLK, 2)
        real_real = jnp.dot(masked[0], column[0], preferred_element_type=jnp.float32)
        imag_imag = jnp.dot(masked[1], column[1], preferred_element_type=jnp.float32)
        real_imag = jnp.dot(masked[0], column[1], preferred_element_type=jnp.float32)
        imag_real = jnp.dot(masked[1], column[0], preferred_element_type=jnp.float32)
        return jnp.stack([real_real - imag_imag, real_imag + imag_real])

    columns = lax.map(one_column, jnp.arange(NBLK, dtype=jnp.int32))
    product = jnp.transpose(columns, (1, 2, 0, 3)).reshape(2, ORDER, ORDER).astype(jnp.bfloat16)
    return product, kept_count, kept_total
```

```python
import functools

import jax
import jax.numpy as jnp
from jax import lax
from jax.experimental import pallas as pl
from jax.experimental.pallas import tpu as pltpu
from jax.sharding import PartitionSpec as P


BLK = 128
GROUP = 4
ANY = pl.BlockSpec(memory_space=pl.ANY)
SMEM = pl.BlockSpec(memory_space=pltpu.SMEM)


def level_scale(levels):
    power = jnp.power(jnp.float32(2.0), (1 - levels).astype(jnp.float32))
    return jnp.where(levels > 0, power, jnp.float32(0.0))


def as_real(block):
    real, imag = block[0], block[1]
    return jnp.concatenate(
        [jnp.concatenate([real, imag], 1), jnp.concatenate([-imag, real], 1)], 0
    )


def add_block(acc, left, block, scales, base, row_blocks):
    added = jnp.dot(left[...], as_real(block), preferred_element_type=jnp.float32)
    for i in range(row_blocks):
        rows = pl.ds(i * BLK, BLK)
        acc[rows, :] += added[i * BLK : (i + 1) * BLK] * scales[base + i]


def pair_copies(source, column, target, sem):
    return [
        pltpu.make_async_copy(
            source.at[part, :, pl.ds(column, BLK)],
            target.at[:, pl.ds(part * BLK, BLK)],
            sem.at[part],
        )
        for part in range(2)
    ]


def dense_kernel(row_blocks, k_blocks, scales, wanted, a_ref, b_ref, out_ref, left, acc, sem):
    j = pl.program_id(0)

    @pl.when(j == 0)
    def _():
        for k in range(k_blocks):
            for copy in pair_copies(a_ref, k * BLK, left.at[k], sem.at[k]):
                copy.start()
        for k in range(k_blocks):
            for copy in pair_copies(a_ref, k * BLK, left.at[k], sem.at[k]):
                copy.wait()

    acc[...] = jnp.zeros_like(acc)

    @pl.loop(0, k_blocks)
    def _(k):
        at = j * k_blocks + k

        @pl.when(wanted[at] > 0)
        def _():
            block = b_ref.at[:, pl.ds(pl.multiple_of(k * BLK, BLK), BLK), :]
            add_block(acc, left.at[k], block[...], scales, at * row_blocks, row_blocks)

    out_ref[0] = acc[:, :BLK].astype(out_ref.dtype)
    out_ref[1] = acc[:, BLK:].astype(out_ref.dtype)


def dense_product(a_whole, b_whole, scale):
    cols, k_blocks, row_blocks = scale.shape
    rows = row_blocks * BLK
    wanted = jnp.any(scale > 0, axis=2).astype(jnp.int32).reshape(-1)
    return pl.pallas_call(
        functools.partial(dense_kernel, row_blocks, k_blocks),
        out_shape=jax.ShapeDtypeStruct((2, rows, cols * BLK), jnp.bfloat16),
        grid=(cols,),
        in_specs=[SMEM, SMEM, ANY, pl.BlockSpec((2, k_blocks * BLK, BLK), lambda j: (0, 0, j))],
        out_specs=pl.BlockSpec((2, rows, BLK), lambda j: (0, 0, j)),
        scratch_shapes=[
            pltpu.VMEM((k_blocks, rows, 2 * BLK), jnp.bfloat16),
            pltpu.VMEM((rows, 2 * BLK), jnp.float32),
            pltpu.SemaphoreType.DMA((k_blocks, 2)),
        ],
        name="dense",
    )(scale.reshape(-1), wanted, a_whole, b_whole)


def pack_kernel(low, lead, row_blocks, with_given, shifted, *refs):
    listed, facts, own = refs[:3]
    given = refs[3] if with_given else None
    out_ref, sem = refs[-2:]
    moved, shift = facts[0], facts[1] * shifted

    def own_copy(q, slot):
        row = pl.multiple_of(lax.rem(slot, row_blocks) * BLK, BLK)
        column = pl.multiple_of(lax.div(slot, row_blocks) * BLK, BLK)
        window = own.at[:, pl.ds(row, BLK), pl.ds(column, BLK)]
        return pltpu.make_async_copy(window, out_ref.at[q], sem.at[q])

    @pl.loop(0, out_ref.shape[0])
    def _(q):
        place = q + low
        if with_given:
            among = (place >= lead) & (place < lead + moved)
            rank = jnp.where(place >= lead, place - moved, place)

            @pl.when(among)
            def _():
                one = given.at[jnp.clip(place - lead, 0, given.shape[0] - 1)]
                pltpu.make_async_copy(one, out_ref.at[q], sem.at[q]).start()

            @pl.when(jnp.logical_not(among))
            def _():
                own_copy(q, listed[jnp.clip(rank, 0, listed.shape[0] - 1)]).start()

        else:
            own_copy(q, listed[jnp.clip(place + shift, 0, listed.shape[0] - 1)]).start()

    @pl.loop(0, out_ref.shape[0])
    def _(q):
        own_copy(q, 0).wait()


def pack(listed, facts, own, given, low, count, lead, row_blocks, shifted):
    operands = [listed, facts, own] + ([] if given is None else [given])
    return pl.pallas_call(
        functools.partial(pack_kernel, low, lead, row_blocks, given is not None, shifted),
        out_shape=jax.ShapeDtypeStruct((count, 2, BLK, BLK), own.dtype),
        in_specs=[SMEM, SMEM] + [ANY] * (len(operands) - 2),
        out_specs=pl.BlockSpec(memory_space=pltpu.VMEM),
        scratch_shapes=[pltpu.SemaphoreType.DMA((count,))],
        cost_estimate=pl.CostEstimate(
            flops=0, transcendentals=0, bytes_accessed=count * 8 * BLK * BLK
        ),
        name="pack",
    )(*operands)


def pick_kernel(ranges, here, *refs):
    out_ref, sem = refs[-2:]
    for act in ("start", "wait"):
        for (low, high), ref in zip(ranges, refs):

            @pl.when((here[0] >= low) & (here[0] <= high))
            def _():
                getattr(pltpu.make_async_copy(ref, out_ref, sem), act)()


def pick(here, ranges, arrays):
    shape = arrays[0].shape
    return pl.pallas_call(
        functools.partial(pick_kernel, ranges),
        out_shape=jax.ShapeDtypeStruct(shape, arrays[0].dtype),
        in_specs=[SMEM] + [ANY] * len(arrays),
        out_specs=pl.BlockSpec(memory_space=pltpu.VMEM),
        scratch_shapes=[pltpu.SemaphoreType.DMA],
        cost_estimate=pl.CostEstimate(
            flops=0, transcendentals=0, bytes_accessed=shape[0] * 8 * BLK * BLK
        ),
        name="pick",
    )(here, *arrays)


def phase_kernel(plan, ranges, with_part, final, *refs):
    slots, row_blocks, sizes = plan
    refs = list(refs)
    take = lambda n: [refs.pop(0) for _ in range(n)]
    facts, starts, lefts, rights, bases, scales = take(6)
    factors = take(3)
    lists = []
    for t in slots:
        choices = [take(len(sizes) - 1) for _ in ranges[t]]
        lists.append((choices, take(1)[0]))
    part_ref = take(1)[0] if with_part else None
    out_ref, left, held, acc, a_sem, b_sem = refs
    j = pl.program_id(0)
    here = facts[0]

    def left_copies(act):
        for n, t in enumerate(slots):
            for which, ref in enumerate(factors):

                @pl.when(facts[1 + 2 * t] == which)
                def _():
                    @pl.loop(0, row_blocks)
                    def _(kk):
                        column = pl.multiple_of((facts[2 + 2 * t] + kk) * BLK, BLK)
                        at = n * row_blocks + kk
                        for copy in pair_copies(ref, column, left.at[at], a_sem.at[at]):
                            act(copy)

    def held_copies(act):
        for n, t in enumerate(slots):
            choices, hop = lists[n]
            at = n * sum(sizes)
            for (low, high), arrays in zip(ranges[t], choices):

                @pl.when((here >= low) & (here <= high))
                def _():
                    for m, array in enumerate(arrays):
                        target = held.at[pl.ds(at + sum(sizes[:m]), sizes[m])]
                        act(pltpu.make_async_copy(array, target, b_sem.at[n, m]))

            m = len(sizes) - 1
            target = held.at[pl.ds(at + sum(sizes[:m]), sizes[m])]
            act(pltpu.make_async_copy(hop, target, b_sem.at[n, m]))

    @pl.when(j == 0)
    def _():
        left_copies(lambda copy: copy.start())
        held_copies(lambda copy: copy.start())
        left_copies(lambda copy: copy.wait())
        held_copies(lambda copy: copy.wait())

    acc[...] = part_ref[0] if with_part else jnp.zeros_like(acc)

    @pl.loop(starts[j], starts[j + 1])
    def _(group):
        entries = [group * GROUP + q for q in range(GROUP)]
        right = jnp.concatenate([as_real(held[rights[e]]) for e in entries], 0)
        scaled = []
        for e in entries:
            factor, base = left[lefts[e]], bases[e]
            rows = [
                factor[i * BLK : (i + 1) * BLK] * scales[base + i].astype(factor.dtype)
                for i in range(row_blocks)
            ]
            scaled.append(jnp.concatenate(rows, 0))
        whole = jnp.concatenate(scaled, 1)
        acc[...] += jnp.dot(whole, right, preferred_element_type=jnp.float32)

    if final:
        out_ref[0] = acc[:, :BLK].astype(out_ref.dtype)
        out_ref[1] = acc[:, BLK:].astype(out_ref.dtype)
    else:
        out_ref[0] = acc[...]


def phase(slots, facts, entries, scales, factors, segments, sizes, ranges, part, final):
    _, rows, width = factors[0].shape
    row_blocks = rows // BLK
    cols = width // BLK
    operands = [facts, *entries, scales] + list(factors)
    loaded = len(operands) - len(factors)
    for t in slots:
        choices, hop = segments[t]
        for arrays in choices:
            operands += arrays
        operands.append(hop)
    specs = [SMEM] * loaded + [ANY] * (len(operands) - loaded)
    if part is not None:
        operands.append(part)
        specs.append(pl.BlockSpec((1, rows, 2 * BLK), lambda j: (j, 0, 0)))
    if final:
        out_shape = jax.ShapeDtypeStruct((2, rows, cols * BLK), factors[0].dtype)
        out_spec = pl.BlockSpec((2, rows, BLK), lambda j: (0, 0, j))
    else:
        out_shape = jax.ShapeDtypeStruct((cols, rows, 2 * BLK), jnp.float32)
        out_spec = pl.BlockSpec((1, rows, 2 * BLK), lambda j: (j, 0, 0))
    plan = (slots, row_blocks, sizes)
    return pl.pallas_call(
        functools.partial(phase_kernel, plan, ranges, part is not None, final),
        out_shape=out_shape,
        grid=(cols,),
        in_specs=specs,
        out_specs=out_spec,
        scratch_shapes=[
            pltpu.VMEM((len(slots) * row_blocks, rows, 2 * BLK), factors[0].dtype),
            pltpu.VMEM((len(slots) * sum(sizes), 2, BLK, BLK), factors[0].dtype),
            pltpu.VMEM((rows, 2 * BLK), jnp.float32),
            pltpu.SemaphoreType.DMA((len(slots) * row_blocks, 2)),
            pltpu.SemaphoreType.DMA((len(slots), len(sizes))),
        ],
        cost_estimate=pl.CostEstimate(
            flops=4 * len(slots) * rows * rows * cols * BLK,
            transcendentals=0,
            bytes_accessed=64 * rows * rows,
        ),
        name="phase",
    )(*operands)


def ranks(flags):
    size = flags.shape[-1]
    before = jnp.arange(size)[:, None] < jnp.arange(size)[None, :]
    set_before = jnp.sum(flags[..., :, None] & before, axis=-2, dtype=jnp.int32)
    return set_before, jnp.sum(flags, axis=-1, dtype=jnp.int32)


def compacted(flags, rank, values):
    hit = flags[..., None, :] & (rank[..., None, :] == jnp.arange(flags.shape[-1])[:, None])
    return jnp.sum(jnp.where(hit, values[..., None, :], 0), axis=-1, dtype=jnp.int32)


def entry_lists(flags, lefts, rights, bases, nothing):
    cols, among = flags.shape
    within, counts = ranks(flags)
    groups = (counts + GROUP - 1) // GROUP
    first = jnp.arange(cols)[:, None] > jnp.arange(cols)[None, :]
    starts = jnp.sum(first * groups[None, :], axis=1, dtype=jnp.int32)
    room = cols * among
    spot = (GROUP * starts[:, None] + within).reshape(-1)
    hit = flags.reshape(-1)[None] & (spot[None] == jnp.arange(room)[:, None])
    listed = lambda values, empty: empty + jnp.sum(
        jnp.where(hit, values.reshape(-1)[None] - empty, 0), axis=1, dtype=jnp.int32
    )
    starts = jnp.concatenate([starts, jnp.sum(groups, dtype=jnp.int32)[None]])
    return starts, listed(lefts, 0), listed(rights, 0), listed(bases, nothing)


def ring(nrow, step):
    return [(i, (i + step) % nrow) for i in range(nrow)]


def listed_product(a_matrix, b_matrix, b_level, scale, nrow, kept):
    row = lax.axis_index("row")
    col = lax.axis_index("col")
    cols, _, row_blocks = scale.shape
    wide = cols * row_blocks
    lead = 5 * wide // 16
    spare = 7 * wide // 32
    rest = wide // 16
    sizes = (lead, spare, rest, spare)
    room = lead + spare + rest

    by_place = b_level.reshape(nrow, row_blocks, 2, cols).transpose(2, 0, 3, 1) > 0
    occupied = by_place.reshape(2, nrow, wide)
    rank, counts = ranks(occupied)
    moved = jnp.clip((counts[1] - counts[0]) // 2, 0, spare)
    light = jnp.where(moved > 0, jnp.maximum(counts[0], lead) + moved, counts[0])
    heavy = counts[1] - moved
    too_long = jnp.any((light > room) | (heavy > room))

    ranges = {t: [(t, nrow - 1)] + [(r, r) for r in range(t)] for t in range(nrow)}

    own_rank = lax.dynamic_slice(rank, (col, row, 0), (1, 1, wide))[0, 0]
    own_set = lax.dynamic_slice(occupied, (col, row, 0), (1, 1, wide))[0, 0]
    listed = compacted(own_set, own_rank, jnp.arange(wide))
    zero = jnp.zeros((), jnp.int32)
    pack_facts = jnp.stack([jnp.where(col == 0, moved[row], zero), heavy[row]])
    packed = functools.partial(pack, listed, pack_facts, b_matrix)

    steps = jnp.arange(nrow)
    source = jnp.where(steps <= row, row - steps, steps)
    rank_here = rank[col][source]
    moved_here = moved[source][:, None]
    heavy_here = heavy[source][:, None]
    first_side = jnp.where(rank_here < lead, rank_here, rank_here + moved_here)
    last_side = jnp.where(rank_here < heavy_here, rank_here, room + rank_here - heavy_here)
    place = jnp.where(col == 0, first_side, last_side).reshape(nrow, cols, row_blocks)
    by_source = scale.reshape(cols, nrow, row_blocks, row_blocks)[:, source].transpose(1, 0, 2, 3)
    wanted = jnp.any(by_source > 0, axis=3)
    nothing = nrow * wide * row_blocks
    scales = jnp.concatenate([by_source.reshape(-1), jnp.zeros((row_blocks,), jnp.float32)])
    bases = (jnp.arange(nrow * wide) * row_blocks).reshape(nrow, cols, row_blocks)
    start = source * row_blocks
    which = jnp.where(start // cols == col, 0, jnp.where(col == 1, 1, 2))
    facts = jnp.concatenate([row[None], jnp.stack([which, start % cols], 1).reshape(-1)])
    facts = facts.astype(jnp.int32)
    held_room = sum(sizes)

    def entries_of(slots):
        at = jnp.array(slots)
        among = jnp.arange(len(slots))[:, None, None]
        across = lambda x: x.transpose(1, 0, 2).reshape(cols, -1)
        lefts = jnp.broadcast_to(among * row_blocks + jnp.arange(row_blocks), place[at].shape)
        rights = jnp.clip(place, 0, held_room - 1)[at] + among * held_room
        return entry_lists(
            across(wanted[at]), across(lefts), across(rights), across(bases[at]), nothing
        )

    plans = [(0, 1)] + [(t,) for t in range(2, nrow)]
    lists = [entries_of(slots) for slots in plans]

    def chunk(given, low, size, shifted=0):
        return packed(given, low, size, lead, row_blocks, shifted)

    def move(array, axis, pairs):
        return lax.ppermute(array, axis, pairs)

    def forward(t, m):
        rises = [(i, i + 1) for i in range(t - 1, nrow - 1)]
        falls = [(i + 1, i) for i in range(nrow - t)]
        up[t][m] = move(up[t - 1][m], "row", rises)
        down[t][m] = move(down[t - 1][m], "row", falls)

    up = [[None] * 3 for _ in range(nrow)]
    down = [[None] * 3 for _ in range(nrow)]
    hops = [None] * nrow

    def hop(t):
        choices = [up[t][1]] + [down[t - r][1] for r in range(t)]
        chosen = pick(row[None].astype(jnp.int32), ranges[t], choices)
        if t == nrow - 2:
            nonlocal facts, scales, lists
            held = (chosen, facts, scales, lists)
            chosen, facts, scales, lists = lax.optimization_barrier(held)
        hops[t] = move(chosen, "col", [(0, 1)])

    a_first = move(a_matrix, "col", [(0, 1)])
    up[0][0] = down[0][0] = chunk(None, 0, lead)
    forward(1, 0)
    hops[0] = chunk(None, 0, spare, 1)
    given = move(hops[0], "col", [(1, 0)])
    up[0][1] = down[0][1] = chunk(given, lead, spare)
    forward(1, 1)
    a_last = move(a_matrix, "col", [(1, 0)])
    up[0][2] = down[0][2] = chunk(given, lead + spare, rest)
    forward(1, 2)
    pair_sum = kept + move(kept, "col", [(0, 1), (1, 0)])
    hop(1)
    for t in range(2, nrow):
        for m in (1, 0, 2):
            forward(t, m)
            if m == 1 and t < nrow - 1:
                hop(t)
        if t == 2:
            kept_total = pair_sum
            for step in range(1, nrow):
                kept_total += move(pair_sum, "row", ring(nrow, step))

    def add(n, part, final):
        slots = plans[n]
        segments = {t: ([up[t]] + [down[t - r] for r in range(t)], hops[t]) for t in slots}
        return phase(slots, facts, lists[n], scales, factors, segments, sizes, ranges, part, final)

    far = nrow - 1
    factors = (a_matrix, a_first, a_last)
    part = add(0, None, False)
    hop(far)
    for n in range(1, len(plans) - 1):
        part = add(n, part, False)

    def all_blocks():
        pieces = [b_matrix]
        for _ in range(1, nrow):
            pieces.append(lax.ppermute(pieces[-1], "row", ring(nrow, 1)))
        b_whole = jnp.stack(pieces)[(row - steps) % nrow].transpose(1, 0, 2, 3)
        b_whole = b_whole.reshape(2, -1, b_matrix.shape[2])
        a_whole = jnp.where(
            col == 0,
            jnp.concatenate([a_matrix, a_last], 2),
            jnp.concatenate([a_first, a_matrix], 2),
        )
        return dense_product(a_whole, b_whole, scale)

    def listed_blocks():
        return add(len(plans) - 1, part, True)

    return lax.cond(too_long, all_blocks, listed_blocks), kept_total


def shards(nrow, in_pairs, a_matrix, b_matrix, a_level, b_level, limit):
    row = lax.axis_index("row")
    col = lax.axis_index("col")
    row_blocks, cols = limit.shape
    a_here = lax.dynamic_slice_in_dim(a_level, row * row_blocks, row_blocks, 0)
    b_here = lax.dynamic_slice_in_dim(b_level, col * cols, cols, 1)
    left = a_here.T[None]
    right = b_here.T[:, :, None]
    keep = (left > 0) & (right > 0) & (left + right <= limit.T[:, None, :])
    kept_count = jnp.sum(keep, axis=1, dtype=jnp.int32).T
    kept = jnp.sum(kept_count).reshape(1)
    scale = jnp.where(keep, level_scale(left) * level_scale(right), jnp.float32(0.0))
    if in_pairs:
        product, kept_total = listed_product(a_matrix, b_matrix, b_level, scale, nrow, kept)
    else:
        a_whole = lax.all_gather(a_matrix, "col", axis=2, tiled=True)
        b_whole = lax.all_gather(b_matrix, "row", axis=1, tiled=True)
        product = dense_product(a_whole, b_whole, scale)
        kept_total = lax.psum(kept, ("row", "col"))
    return (product, kept_count, kept_total)


def solution(mesh):
    in_specs = (
        P("kpt", "row", "col"),
        P("kpt", "row", "col"),
        P("kpt", None),
        P("kpt", None),
        P(("kpt", "row"), "col"),
    )
    out_specs = (P("kpt", "row", "col"), P(("kpt", "row"), "col"), P("kpt"))
    nrow, ncol = mesh.shape["row"], mesh.shape["col"]
    in_pairs = ncol == 2 and nrow > 2

    def body(*args):
        return shards(nrow, in_pairs, *args)

    return jax.shard_map(body, mesh=mesh, in_specs=in_specs, out_specs=out_specs, check_vma=False)
```
